128 devices in a mesh: ckpt: 8 (over x_lo, z), shard: 16 (over x_hi, y, core).
Axes of the slice: x: 4 (x_hi: 2, x_lo: 2; x = x_hi * 2 + x_lo), y: 4, z: 4, core: 2. Of those that a mesh axis runs over, the one named last changes fastest.
Arguments:
- task_vectors: bfloat16 [8, 4096, 16384], P('ckpt', 'shard'), may hold values from -0.125 to 0.125, as said below
- thresholds: float32 [8], replicated, may hold values from 0.009 to 0.062, as said below
- base_weight: float32 [4096, 16384], P('ckpt', 'shard'), may hold values from -0.3 to 0.3
Outputs:
- merged: float32 [4096, 16384], P('ckpt', 'shard')
The draws below stay inside these ranges and needn't reach their ends.
Inputs may be any that keep to these rules, and one draw needn't show every extreme that they name: `task_vectors`: every entry is a whole multiple of 2^-14. `thresholds`: every threshold is an odd multiple of 2^-15.
All inputs are finite; a program needn't handle non-finite values.
Results may differ from the reference program's by a relative error of at most 0.0003.
Values may be sent and summed in bfloat16 or wider, within the bound.
No kernel may reach another device: no remote copies, remote signals or barrier semaphores. Data moves between devices by JAX's collectives and lax.ppermute only.
A program may use at most 128 MiB of HBM per device.

```python
import jax
import jax.numpy as jnp
from jax import lax

D = 4096
FFW = 16384
TASKS = 8


def draw_task_vectors(key, part):
    first_key, second_key = jax.random.split(key, 2)
    steps_count = jax.random.randint(first_key, (TASKS, D, FFW), -255, 256)
    exponent = jax.random.randint(second_key, (TASKS, D, FFW), 0, 4)
    values = steps_count.astype(jnp.float32) * jnp.exp2(exponent.astype(jnp.float32) - 14.0)
    return values.astype(jnp.bfloat16)


def draw_thresholds(key, part):
    middle = jax.random.randint(jax.random.fold_in(key, 11), (TASKS,), 160, 1000)
    return (2 * middle + 1).astype(jnp.float32) / 32768.0


def levels(key, dims, cuts, low, largest):
    level, own = 1.0, jax.random.fold_in(key, 6)
    for axis_at, blocks in cuts:
        draws = jnp.exp(jax.random.uniform(jax.random.fold_in(own, axis_at), (blocks,), jnp.float32, low / len(cuts), largest / len(cuts)))
        level = level * jnp.repeat(draws, dims[axis_at] // blocks).reshape([-1 if axis == axis_at else 1 for axis in range(len(dims))])
    return level


def normal_values(stream_key, extent, deviation, most, shards=(), kind=jnp.bfloat16):
    factor_of = levels(stream_key, extent, shards, -0.22, 0.18) if shards else 1.0
    values = jax.random.normal(stream_key, extent, jnp.float32) * deviation * factor_of
    return jnp.minimum(jnp.maximum(values, -most), most).astype(kind)


def setup_inputs(seed: int = 0) -> dict:
    splits = jax.random.split(jax.random.key(seed), 4)
    task_vectors = draw_task_vectors(jax.random.fold_in(splits[3], 71), 0)
    thresholds = draw_thresholds(jax.random.fold_in(splits[3], 71), 0)
    base_weight = normal_values(splits[2], (D, FFW), 0.05, 0.3, ((0, 8), (1, 16)), jnp.float32)
    return dict(task_vectors=task_vectors, thresholds=thresholds, base_weight=base_weight)


def trim_values(task_block, limit_value):
    values = task_block.astype(jnp.float32)
    return jnp.where(jnp.abs(values) > limit_value, values, jnp.float32(0.0))


def reference(task_vectors, thresholds, base_weight):
    def add_trimmed(running, inputs):
        return running + trim_values(inputs[0], inputs[1]), None

    zeros_block = jnp.zeros(base_weight.shape, jnp.float32)
    signed_total, unused = lax.scan(add_trimmed, zeros_block, (task_vectors, thresholds))

    def add_agreeing(running, inputs):
        trimmed = trim_values(inputs[0], inputs[1])
        agreeing = jnp.logical_or(jnp.logical_and(signed_total > 0, trimmed > 0),
                                  jnp.logical_and(signed_total < 0, trimmed < 0))
        kept_sum = running[0] + jnp.where(agreeing, trimmed, jnp.float32(0.0))
        agree_count = running[1] + agreeing.astype(jnp.float32)
        return (kept_sum, agree_count), None

    (kept_sum, agree_count), unused = lax.scan(add_agreeing, (zeros_block, zeros_block), (task_vectors, thresholds))
    disjoint = jnp.where(agree_count > 0, kept_sum / jnp.maximum(agree_count, 1.0), jnp.float32(0.0))
    return base_weight + disjoint
```

```python
import functools

import jax
import jax.numpy as jnp
from jax import lax
from jax.experimental import pallas as pl
from jax.experimental.pallas import tpu as pltpu
from jax.sharding import PartitionSpec as P

AXES = ("ckpt", "shard")
CHUNKS = (208, 48)
LIFT = 4.0
SCALE, SHIFT = 1920.0, -120.0
BLOCK_ROWS = 16
SLICE = 128


def number(x, y, z, c):
    return ((x % 2) * 4 + z % 4) * 16 + ((x // 2) * 4 + y % 4) * 2 + c


PLACES = [(x, y, z, c) for x in range(4) for y in range(4) for z in range(4) for c in range(2)]


def pairs(target):
    return [(number(*p), number(*target(*p))) for p in PLACES]


def column_x(x_lo, c):
    return x_lo ^ c


def column_y(y, z, c):
    return (z - y + 2 * c + 4) % 4


def home(half):
    return lambda x, y, z, c: (x // 2 + 2 * column_x(x % 2, c), column_y(y, z, c), y, c ^ half)


def pack_kernel(at, order, own, out, sems):
    count, rows, width = out.shape
    copies = []
    for i in range(count):
        column = pl.multiple_of(order[i] * width, width)
        copies.append(pltpu.make_async_copy(own.at[pl.ds(at, rows), pl.ds(column, width)], out.at[i], sems.at[i]))
    for copy in copies:
        copy.start()
    for copy in copies:
        copy.wait()


def packed(own, order, at, rows):
    width = own.shape[1] // 8
    return pl.pallas_call(
        functools.partial(pack_kernel, at),
        in_specs=[pl.BlockSpec(memory_space=pltpu.SMEM), pl.BlockSpec(memory_space=pltpu.HBM)],
        out_specs=pl.BlockSpec(memory_space=pl.ANY),
        scratch_shapes=[pltpu.SemaphoreType.DMA((8,))],
        out_shape=OUT((8, rows, width), own.dtype),
        compiler_params=pltpu.CompilerParams(vmem_limit_bytes=2**20),
        name="pack",
    )(order, own)


OUT = jax.ShapeDtypeStruct


def coded(mean):
    size = jnp.exp2(jnp.abs(mean) * SCALE + SHIFT)
    return jnp.where(mean < 0, -size, size).astype(jnp.bfloat16)


def decoded(code):
    code = code.astype(jnp.float32)
    size = jnp.abs(code)
    mean = (jnp.log2(size) - SHIFT) * (1.0 / SCALE)
    mean = jnp.where(size > 2.0 ** (SHIFT + 1), mean, 0.0)
    return jnp.where(code < 0, -mean, mean)


def mean_kernel(core, limits, tasks_same, tasks_other, same, other):
    for tasks, out in ((tasks_same, same), (tasks_other, other)):
        for first in range(0, out.shape[1], SLICE):
            high = jnp.zeros((BLOCK_ROWS, SLICE), jnp.float32)
            low = jnp.zeros((BLOCK_ROWS, SLICE), jnp.float32)
            for t in range(8):
                value = tasks[t, :, first : first + SLICE].astype(jnp.float32)
                limit = limits[t]
                high = high + jnp.where(value > limit, value + LIFT, 0.0)
                low = low + jnp.where(value < -limit, value - LIFT, 0.0)
            high_count = jnp.floor(high * (1.0 / LIFT))
            low_count = jnp.floor(low * (-1.0 / LIFT))
            high_sum = high - LIFT * high_count
            low_sum = low + LIFT * low_count
            total = high_sum + low_sum
            kept = jnp.where(total > 0, high_sum, low_sum)
            count = jnp.where(total > 0, high_count, low_count)
            mean = jnp.where(total != 0, kept / jnp.maximum(count, 1.0), 0.0)
            out[:, first : first + SLICE] = coded(mean)


def disjoint_mean(tasks, limits, core):
    count, rows, width = tasks.shape
    out = jax.ShapeDtypeStruct((rows, width // 2), jnp.bfloat16)
    block = pl.BlockSpec((BLOCK_ROWS, width // 2), lambda r, *_: (r, 0))
    return pl.pallas_call(
        mean_kernel,
        grid_spec=pltpu.PrefetchScalarGridSpec(
            num_scalar_prefetch=2,
            grid=(rows // BLOCK_ROWS,),
            in_specs=[
                pl.BlockSpec((count, BLOCK_ROWS, width // 2), lambda r, core, limits: (0, r, core[0])),
                pl.BlockSpec((count, BLOCK_ROWS, width // 2), lambda r, core, limits: (0, r, 1 - core[0])),
            ],
            out_specs=[block, block],
        ),
        out_shape=[out, out],
        compiler_params=pltpu.CompilerParams(vmem_limit_bytes=16 * 2**20),
        name="mean",
    )(core, limits, tasks, tasks)


def local(task_vectors, thresholds, base_weight):
    own = task_vectors[0]
    shard = lax.axis_index("shard")
    y, c = (shard // 2) % 4, shard % 2
    core = c[None].astype(jnp.int32)
    place = jnp.arange(8, dtype=jnp.int32)
    order = column_x(place // 4, c) * 4 + column_y(y, place % 4, c)
    at, same, other = 0, [], []
    for rows in CHUNKS:
        blocks = packed(own, order, at, rows)
        tasks = lax.all_to_all(blocks, "ckpt", split_axis=0, concat_axis=0, tiled=True)
        code_same, code_other = disjoint_mean(tasks, thresholds, core)
        same.append(lax.ppermute(code_same, AXES, pairs(home(0))))
        other.append(lax.ppermute(code_other, AXES, pairs(home(1))))
        at += rows
    same, other = jnp.concatenate(same), jnp.concatenate(other)
    first = jnp.where(c == 0, same, other)
    second = jnp.where(c == 0, other, same)
    return base_weight + decoded(jnp.concatenate([first, second]))


def solution(mesh):
    placed = (P("ckpt", "shard", None), P(), P("ckpt", "shard"))
    return jax.shard_map(
        local, mesh=mesh, in_specs=placed, out_specs=P("ckpt", "shard"), check_vma=False
    )
```

```python
import functools

import jax
import jax.numpy as jnp
from jax import lax
from jax.experimental import pallas as pl
from jax.experimental.pallas import tpu as pltpu
from jax.sharding import Mesh, PartitionSpec as P

SIZES = dict(x_lo=2, z=4, x_hi=2, y=4, core=2)
AXES = tuple(SIZES)
CHUNKS = (192, 64)
STEPS = ((1, 0), (3, 1), (2, 0), (1, 1), (3, 0), (2, 1), (0, 1))
EARLY, GATE_ON = (5,), 4
AHEAD = 8
LIFT = 4.0
SCALE, SHIFT = 1920.0, -120.0
BLOCK_ROWS, ADD_ROWS = 64, 64
TILE_ROWS, SLICE = 16, 128


def columns_of(x_lo, y, z, core):
    return x_lo, (z - y + 2 * core + 4) % 4


def moved(x_lo, z, core, hops, flip):
    return x_lo ^ flip, (z + hops * (1 - 2 * core) + 4) % 4


def meet(hops, flip):
    def target(x_lo, z, x_hi, y, core):
        return *moved(x_lo, z, core, hops, flip), x_hi, y, core

    return target


def home(half):
    def target(x_lo, z, x_hi, y, core):
        return x_hi, y, *columns_of(x_lo, y, z, core), core ^ half

    return target


def number(place):
    at = 0
    for index, size in zip(place, SIZES.values()):
        at = at * size + index
    return at


def pairs(target):
    places = [()]
    for size in SIZES.values():
        places = [place + (index,) for place in places for index in range(size)]
    return [(number(place), number(target(*place))) for place in places]


def pack_kernel(at, order, own, out, held, came, went):
    count, rows, width = out.shape
    loads, stores = [], []
    for i in range(count):
        column = pl.multiple_of(order[i] * width, width)
        loads.append(pltpu.make_async_copy(own.at[pl.ds(at, rows), pl.ds(column, width)], held.at[i], came.at[i]))
        stores.append(pltpu.make_async_copy(held.at[i], out.at[i], went.at[i]))
    for load in loads[:AHEAD]:
        load.start()
    for i, (load, store) in enumerate(zip(loads, stores)):
        load.wait()
        store.start()
        if i + AHEAD < count:
            loads[i + AHEAD].start()
    for store in stores:
        store.wait()


def packed(own, order, at, rows):
    count = order.shape[0]
    shape = (count, rows, own.shape[1] // count)
    return pl.pallas_call(
        functools.partial(pack_kernel, at),
        in_specs=[pl.BlockSpec(memory_space=pltpu.SMEM), pl.BlockSpec(memory_space=pl.ANY)],
        out_specs=pl.BlockSpec(memory_space=pl.ANY),
        scratch_shapes=[
            pltpu.VMEM(shape, own.dtype),
            pltpu.SemaphoreType.DMA((count,)),
            pltpu.SemaphoreType.DMA((count,)),
        ],
        out_shape=jax.ShapeDtypeStruct(shape, own.dtype),
        compiler_params=pltpu.CompilerParams(vmem_limit_bytes=60 * 2**20),
        name="pack",
    )(order, own)


def coded(mean):
    size = jnp.exp2(jnp.abs(mean) * SCALE + SHIFT)
    return jnp.where(mean < 0, -size, size).astype(jnp.bfloat16)


def decoded(code):
    code = code.astype(jnp.float32)
    size = jnp.abs(code)
    mean = (jnp.log2(size) - SHIFT) * (1.0 / SCALE)
    mean = jnp.where(size > 2.0 ** (SHIFT + 1), mean, 0.0)
    return jnp.where(code < 0, -mean, mean)


def merged_tile(values, limits):
    high = low = None
    for value, limit in zip(values, limits):
        lifted = value + LIFT
        above = jnp.where(value > limit, lifted, 0.0)
        below = jnp.where(value < -limit, lifted, 0.0)
        high = above if high is None else high + above
        low = below if low is None else low + below
    high_count = jnp.floor(high * (1.0 / LIFT))
    low_count = jnp.ceil(low * (1.0 / LIFT))
    high_sum = high - LIFT * high_count
    low_sum = low - LIFT * low_count
    total = high_sum + low_sum
    kept = jnp.where(total > 0, high_sum, low_sum)
    count = jnp.where(total > 0, high_count, low_count)
    return jnp.where(total != 0, kept / jnp.maximum(count, 1.0), 0.0)


def mean_kernel(core, limits, tasks_same, tasks_other, same, other):
    for tasks, out in ((tasks_same, same), (tasks_other, other)):
        for row in range(0, out.shape[0], TILE_ROWS):
            for column in range(0, out.shape[1], SLICE):
                tile = pl.ds(row, TILE_ROWS), pl.ds(column, SLICE)
                values = [tasks[(t, *tile)].astype(jnp.float32) for t in range(tasks.shape[0])]
                out[tile] = coded(merged_tile(values, [limits[t] for t in range(len(values))]))


def coded_mean(tasks, limits, core):
    count, rows, width = tasks.shape
    out = jax.ShapeDtypeStruct((rows, width // 2), jnp.bfloat16)
    block = pl.BlockSpec((BLOCK_ROWS, width // 2), lambda r, *_: (r, 0))
    half = (count, BLOCK_ROWS, width // 2)
    return pl.pallas_call(
        mean_kernel,
        grid_spec=pltpu.PrefetchScalarGridSpec(
            num_scalar_prefetch=2,
            grid=(rows // BLOCK_ROWS,),
            in_specs=[
                pl.BlockSpec(half, lambda r, core, limits: (0, r, core[0])),
                pl.BlockSpec(half, lambda r, core, limits: (0, r, 1 - core[0])),
            ],
            out_specs=[block, block],
        ),
        out_shape=[out, out],
        compiler_params=pltpu.CompilerParams(vmem_limit_bytes=16 * 2**20),
        name="mean",
    )(core, limits, tasks, tasks)


def blocks_kernel(core, source, thresholds, *refs):
    blocks, outs = refs[:8], refs[8:]
    width = outs[0].shape[1]
    limits = [thresholds[source[i]] for i in range(8)]
    for half, out in enumerate(outs):
        for row in range(0, out.shape[0], TILE_ROWS):
            for first in range(0, width, SLICE):
                at = pl.multiple_of((core[0] ^ half) * width + first, SLICE)
                values = [block[pl.ds(row, TILE_ROWS), pl.ds(at, SLICE)].astype(jnp.float32) for block in blocks]
                out[pl.ds(row, TILE_ROWS), pl.ds(first, SLICE)] = coded(merged_tile(values, limits))


def coded_mean_of(blocks, source, thresholds, core):
    rows, width = blocks[0].shape
    out = jax.ShapeDtypeStruct((rows, width // 2), jnp.bfloat16)
    unit = min(rows, BLOCK_ROWS)
    block = pl.BlockSpec((unit, width), lambda r, *_: (r, 0))
    return pl.pallas_call(
        blocks_kernel,
        grid_spec=pltpu.PrefetchScalarGridSpec(
            num_scalar_prefetch=3,
            grid=(rows // unit,),
            in_specs=[block] * 8,
            out_specs=[pl.BlockSpec((unit, width // 2), lambda r, *_: (r, 0))] * 2,
        ),
        out_shape=[out, out],
        compiler_params=pltpu.CompilerParams(vmem_limit_bytes=16 * 2**20),
        name="mean_of_blocks",
    )(core, source, thresholds, *blocks)


def add_kernel(core, base, same, other, *rest):
    out = rest[-1]

    @pl.when(pl.program_id(0) == 0)
    def _():
        out[...] = base[...] + decoded(same[...])

    @pl.when(pl.program_id(0) == 1)
    def _():
        out[...] = base[...] + decoded(other[...])


def added(core, base, same, other, at, partial):
    rows, width = same.shape
    unit = ADD_ROWS
    halves = base.shape[0] // 2 // unit
    whole = pl.BlockSpec((unit, width), lambda h, r, core: ((h ^ core[0]) * halves + at // unit + r, 0))
    last = rows // unit - 1
    in_specs = [
        whole,
        pl.BlockSpec((unit, width), lambda h, r, core: (r * (1 - h) + last * h, 0)),
        pl.BlockSpec((unit, width), lambda h, r, core: (r * h, 0)),
    ]
    args = [core, base, same, other]
    aliases = {}
    if partial is not None:
        in_specs.append(pl.BlockSpec(memory_space=pl.ANY))
        args.append(partial)
        aliases = {4: 0}
    return pl.pallas_call(
        add_kernel,
        grid_spec=pltpu.PrefetchScalarGridSpec(
            num_scalar_prefetch=1, grid=(2, rows // unit), in_specs=in_specs, out_specs=whole
        ),
        out_shape=jax.ShapeDtypeStruct(base.shape, base.dtype),
        input_output_aliases=aliases,
        compiler_params=pltpu.CompilerParams(vmem_limit_bytes=16 * 2**20),
        name="add",
    )(*args)


def local(task_vectors, thresholds, base_weight):
    own = task_vectors[0]
    width = own.shape[1] // 8
    x_lo, z, y, core = (lax.axis_index(name) for name in ("x_lo", "z", "y", "core"))
    place = jnp.arange(8, dtype=jnp.int32)
    to_x_hi, to_y = columns_of(place // 4, y, place % 4, core)
    order = to_x_hi * 4 + to_y
    one = core[None].astype(jnp.int32)

    def column(hops, flip):
        to_x_lo, to_z = moved(x_lo, z, core, hops, flip)
        to_x_hi, to_y = columns_of(to_x_lo, y, to_z, core)
        return to_x_hi * 4 + to_y

    def source(hops, flip):
        from_x_lo, from_z = moved(x_lo, z, core, 4 - hops, flip)
        return from_x_lo * 4 + from_z

    sources = jnp.stack([source(*step) for step in ((0, 0), *STEPS)])

    def send(block, step):
        return lax.ppermute(block, AXES, pairs(meet(*step)))

    def send_home(codes):
        return [lax.ppermute(code, AXES, pairs(home(half))) for half, code in enumerate(codes)]

    starts = [sum(CHUNKS[:i]) for i in range(len(CHUNKS))]
    tasks = lax.all_to_all(
        packed(own, order, 0, CHUNKS[0]), ("x_lo", "z"), split_axis=0, concat_axis=0, tiled=True
    )
    blocks = [
        [lax.dynamic_slice(own, (at, column(*step) * width), (rows, width)) for step in ((0, 0), *STEPS)]
        for at, rows in zip(starts[1:], CHUNKS[1:])
    ]
    codes = coded_mean(tasks, thresholds, one)
    arrived, homes = None, []
    for here, early in zip(blocks, EARLY):
        if arrived is not None:
            here[1:], arrived[GATE_ON] = lax.optimization_barrier((here[1:], arrived[GATE_ON]))
            codes = coded_mean_of(arrived, sources, thresholds, one)
        sent = [send(block, step) for block, step in zip(here[1 : 1 + early], STEPS)]
        late, codes = lax.optimization_barrier((here[1 + early :], codes))
        homes.append(send_home(codes))
        arrived = here[:1] + sent + [send(block, step) for block, step in zip(late, STEPS[early:])]
    codes = coded_mean_of(arrived, sources, thresholds, one)
    homes.append(send_home(codes))
    out = None
    for (same, other), at in zip(homes, starts):
        out = added(one, base_weight, same, other, at, out)
    return out


def solution(mesh):
    finer = Mesh(mesh.devices.reshape(tuple(SIZES.values())), AXES)
    ckpt, shard = ("x_lo", "z"), ("x_hi", "y", "core")
    return jax.shard_map(
        local,
        mesh=finer,
        in_specs=(P(ckpt, shard, None), P(), P(ckpt, shard)),
        out_specs=P(ckpt, shard),
        check_vma=False,
    )
```

```python
import functools

import jax
import jax.numpy as jnp
from jax import lax
from jax.experimental import pallas as pl
from jax.experimental.pallas import tpu as pltpu
from jax.sharding import Mesh, PartitionSpec as P

SIZES = dict(x_lo=2, z=4, x_hi=2, y=4, core=2)
AXES = tuple(SIZES)
CHUNKS = (160, 96)
STEPS = ((1, 0), (3, 1), (2, 0), (1, 1), (3, 0), (2, 1), (0, 1))
EARLY, GATE_ON = (4,), 4
AHEAD = 8
LIFT = 4.0
SCALE, SHIFT = 1920.0, -120.0
BLOCK_ROWS, BLOCK_ROWS_B, ADD_ROWS = 80, 48, (80, 96)
TILE_ROWS, SLICE = 16, 128


def columns_of(x_lo, y, z, core):
    return x_lo, (z - y + 2 * core + 4) % 4


def moved(x_lo, z, core, hops, flip):
    return x_lo ^ flip, (z + hops * (1 - 2 * core) + 4) % 4


def meet(hops, flip):
    def target(x_lo, z, x_hi, y, core):
        return *moved(x_lo, z, core, hops, flip), x_hi, y, core

    return target


def home(half):
    def target(x_lo, z, x_hi, y, core):
        return x_hi, y, *columns_of(x_lo, y, z, core), core ^ half

    return target


def number(place):
    at = 0
    for index, size in zip(place, SIZES.values()):
        at = at * size + index
    return at


def pairs(target):
    places = [()]
    for size in SIZES.values():
        places = [place + (index,) for place in places for index in range(size)]
    return [(number(place), number(target(*place))) for place in places]


def pack_kernel(at, order, own, out, held, came, went):
    count, rows, width = out.shape
    loads, stores = [], []
    for i in range(count):
        column = pl.multiple_of(order[i] * width, width)
        loads.append(pltpu.make_async_copy(own.at[pl.ds(at, rows), pl.ds(column, width)], held.at[i], came.at[i]))
        stores.append(pltpu.make_async_copy(held.at[i], out.at[i], went.at[i]))
    for load in loads[:AHEAD]:
        load.start()
    for i, (load, store) in enumerate(zip(loads, stores)):
        load.wait()
        store.start()
        if i + AHEAD < count:
            loads[i + AHEAD].start()
    for store in stores:
        store.wait()


def packed(own, order, at, rows):
    count = order.shape[0]
    shape = (count, rows, own.shape[1] // count)
    return pl.pallas_call(
        functools.partial(pack_kernel, at),
        in_specs=[pl.BlockSpec(memory_space=pltpu.SMEM), pl.BlockSpec(memory_space=pl.ANY)],
        out_specs=pl.BlockSpec(memory_space=pl.ANY),
        scratch_shapes=[
            pltpu.VMEM(shape, own.dtype),
            pltpu.SemaphoreType.DMA((count,)),
            pltpu.SemaphoreType.DMA((count,)),
        ],
        out_shape=jax.ShapeDtypeStruct(shape, own.dtype),
        compiler_params=pltpu.CompilerParams(vmem_limit_bytes=60 * 2**20),
        name="pack",
    )(order, own)


def coded(mean):
    size = jnp.exp2(jnp.abs(mean) * SCALE + SHIFT)
    return jnp.where(mean < 0, -size, size).astype(jnp.bfloat16)


def decoded(code):
    code = code.astype(jnp.float32)
    size = jnp.abs(code)
    mean = (jnp.log2(size) - SHIFT) * (1.0 / SCALE)
    mean = jnp.where(size > 2.0 ** (SHIFT + 1), mean, 0.0)
    return jnp.where(code < 0, -mean, mean)


def merged_tile(values, limits):
    high = low = None
    for value, limit in zip(values, limits):
        lifted = value + LIFT
        above = jnp.where(value > limit, lifted, 0.0)
        below = jnp.where(value < -limit, lifted, 0.0)
        high = above if high is None else high + above
        low = below if low is None else low + below
    high_count = jnp.floor(high * (1.0 / LIFT))
    low_count = jnp.ceil(low * (1.0 / LIFT))
    high_sum = high - LIFT * high_count
    low_sum = low - LIFT * low_count
    total = high_sum + low_sum
    kept = jnp.where(total > 0, high_sum, low_sum)
    count = jnp.where(total > 0, high_count, low_count)
    return jnp.where(total != 0, kept / jnp.maximum(count, 1.0), 0.0)


def mean_kernel(core, limits, tasks_same, tasks_other, same, other):
    for tasks, out in ((tasks_same, same), (tasks_other, other)):
        for row in range(0, out.shape[0], TILE_ROWS):
            for column in range(0, out.shape[1], SLICE):
                tile = pl.ds(row, TILE_ROWS), pl.ds(column, SLICE)
                values = [tasks[(t, *tile)].astype(jnp.float32) for t in range(tasks.shape[0])]
                out[tile] = coded(merged_tile(values, [limits[t] for t in range(len(values))]))


def coded_mean(tasks, limits, core):
    count, rows, width = tasks.shape
    out = jax.ShapeDtypeStruct((rows, width // 2), jnp.bfloat16)
    block = pl.BlockSpec((BLOCK_ROWS, width // 2), lambda r, *_: (r, 0))
    half = (count, BLOCK_ROWS, width // 2)
    return pl.pallas_call(
        mean_kernel,
        grid_spec=pltpu.PrefetchScalarGridSpec(
            num_scalar_prefetch=2,
            grid=(rows // BLOCK_ROWS,),
            in_specs=[
                pl.BlockSpec(half, lambda r, core, limits: (0, r, core[0])),
                pl.BlockSpec(half, lambda r, core, limits: (0, r, 1 - core[0])),
            ],
            out_specs=[block, block],
        ),
        out_shape=[out, out],
        compiler_params=pltpu.CompilerParams(vmem_limit_bytes=16 * 2**20),
        name="mean",
    )(core, limits, tasks, tasks)


def blocks_kernel(core, source, thresholds, *refs):
    blocks, outs = refs[:8], refs[8:]
    width = outs[0].shape[1]
    limits = [thresholds[source[i]] for i in range(8)]
    for half, out in enumerate(outs):
        for row in range(0, out.shape[0], TILE_ROWS):
            for first in range(0, width, SLICE):
                at = pl.multiple_of((core[0] ^ half) * width + first, SLICE)
                values = [block[pl.ds(row, TILE_ROWS), pl.ds(at, SLICE)].astype(jnp.float32) for block in blocks]
                out[pl.ds(row, TILE_ROWS), pl.ds(first, SLICE)] = coded(merged_tile(values, limits))


def coded_mean_of(blocks, source, thresholds, core):
    rows, width = blocks[0].shape
    out = jax.ShapeDtypeStruct((rows, width // 2), jnp.bfloat16)
    unit = min(rows, BLOCK_ROWS_B)
    block = pl.BlockSpec((unit, width), lambda r, *_: (r, 0))
    return pl.pallas_call(
        blocks_kernel,
        grid_spec=pltpu.PrefetchScalarGridSpec(
            num_scalar_prefetch=3,
            grid=(rows // unit,),
            in_specs=[block] * 8,
            out_specs=[pl.BlockSpec((unit, width // 2), lambda r, *_: (r, 0))] * 2,
        ),
        out_shape=[out, out],
        compiler_params=pltpu.CompilerParams(vmem_limit_bytes=16 * 2**20),
        name="mean_of_blocks",
    )(core, source, thresholds, *blocks)


def add_kernel(core, base, same, other, *rest):
    out = rest[-1]

    @pl.when(pl.program_id(0) == 0)
    def _():
        out[...] = base[...] + decoded(same[...])

    @pl.when(pl.program_id(0) == 1)
    def _():
        out[...] = base[...] + decoded(other[...])


def added(core, base, same, other, at, partial, unit):
    rows, width = same.shape
    half_rows = base.shape[0] // 2
    steps = rows // unit

    def place(h, r, core):
        return pl.multiple_of((h ^ core[0]) * half_rows + at + r * unit, 8), 0

    whole = pl.BlockSpec((pl.Element(unit), pl.Element(width)), place)
    in_specs = [
        whole,
        pl.BlockSpec((unit, width), lambda h, r, core: (r * (1 - h) + (steps - 1) * h, 0)),
        pl.BlockSpec((unit, width), lambda h, r, core: (r * h, 0)),
    ]
    args = [core, base, same, other]
    aliases = {}
    if partial is not None:
        in_specs.append(pl.BlockSpec(memory_space=pl.ANY))
        args.append(partial)
        aliases = {4: 0}
    return pl.pallas_call(
        add_kernel,
        grid_spec=pltpu.PrefetchScalarGridSpec(
            num_scalar_prefetch=1, grid=(2, steps), in_specs=in_specs, out_specs=whole
        ),
        out_shape=jax.ShapeDtypeStruct(base.shape, base.dtype),
        input_output_aliases=aliases,
        compiler_params=pltpu.CompilerParams(vmem_limit_bytes=16 * 2**20),
        name="add",
    )(*args)


def local(task_vectors, thresholds, base_weight):
    own = task_vectors[0]
    width = own.shape[1] // 8
    x_lo, z, y, core = (lax.axis_index(name) for name in ("x_lo", "z", "y", "core"))
    place = jnp.arange(8, dtype=jnp.int32)
    to_x_hi, to_y = columns_of(place // 4, y, place % 4, core)
    order = to_x_hi * 4 + to_y
    one = core[None].astype(jnp.int32)

    def column(hops, flip):
        to_x_lo, to_z = moved(x_lo, z, core, hops, flip)
        to_x_hi, to_y = columns_of(to_x_lo, y, to_z, core)
        return to_x_hi * 4 + to_y

    def source(hops, flip):
        from_x_lo, from_z = moved(x_lo, z, core, 4 - hops, flip)
        return from_x_lo * 4 + from_z

    sources = jnp.stack([source(*step) for step in ((0, 0), *STEPS)])

    def send(block, step):
        return lax.ppermute(block, AXES, pairs(meet(*step)))

    def send_home(codes):
        return [lax.ppermute(code, AXES, pairs(home(half))) for half, code in enumerate(codes)]

    starts = [sum(CHUNKS[:i]) for i in range(len(CHUNKS))]
    tasks = lax.all_to_all(
        packed(own, order, 0, CHUNKS[0]), ("x_lo", "z"), split_axis=0, concat_axis=0, tiled=True
    )
    blocks = [
        [lax.dynamic_slice(own, (at, column(*step) * width), (rows, width)) for step in ((0, 0), *STEPS)]
        for at, rows in zip(starts[1:], CHUNKS[1:])
    ]
    codes = coded_mean(tasks, thresholds, one)
    arrived, homes = None, []
    for here, early in zip(blocks, EARLY):
        if arrived is not None:
            here[1:], arrived[GATE_ON] = lax.optimization_barrier((here[1:], arrived[GATE_ON]))
            codes = coded_mean_of(arrived, sources, thresholds, one)
        sent = [send(block, step) for block, step in zip(here[1 : 1 + early], STEPS)]
        late, codes = lax.optimization_barrier((here[1 + early :], codes))
        homes.append(send_home(codes))
        arrived = here[:1] + sent + [send(block, step) for block, step in zip(late, STEPS[early:])]
    codes = coded_mean_of(arrived, sources, thresholds, one)
    homes.append(send_home(codes))
    out = None
    for (same, other), at, unit in zip(homes, starts, ADD_ROWS):
        out = added(one, base_weight, same, other, at, out, unit)
    return out


def solution(mesh):
    finer = Mesh(mesh.devices.reshape(tuple(SIZES.values())), AXES)
    ckpt, shard = ("x_lo", "z"), ("x_hi", "y", "core")
    return jax.shard_map(
        local,
        mesh=finer,
        in_specs=(P(ckpt, shard, None), P(), P(ckpt, shard)),
        out_specs=P(ckpt, shard),
        check_vma=False,
    )
```

```python
import functools

import jax
import jax.numpy as jnp
from jax import lax
from jax.experimental import pallas as pl
from jax.experimental.pallas import tpu as pltpu
from jax.sharding import Mesh, PartitionSpec as P

SIZES = dict(x_lo=2, z=4, x_hi=2, y=4, core=2)
AXES = tuple(SIZES)
CHUNKS = (160, 96)
STEPS = ((1, 0), (3, 1), (2, 0), (1, 1), (3, 0), (2, 1), (0, 1))
EARLY, GATE_ON = (4,), 4
AHEAD = 8
LIFT = 4.0
SCALE, SHIFT = 1920.0, -120.0
BLOCK_ROWS, BLOCK_ROWS_B, ADD_ROWS = 40, 48, (160, 96)
TILE_ROWS, SLICE = 8, 128


def columns_of(x_lo, y, z, core):
    return x_lo, (z - y + 2 * core + 4) % 4


def moved(x_lo, z, core, hops, flip):
    return x_lo ^ flip, (z + hops * (1 - 2 * core) + 4) % 4


def meet(hops, flip):
    def target(x_lo, z, x_hi, y, core):
        return *moved(x_lo, z, core, hops, flip), x_hi, y, core

    return target


def home(half):
    def target(x_lo, z, x_hi, y, core):
        return x_hi, y, *columns_of(x_lo, y, z, core), core ^ half

    return target


def number(place):
    at = 0
    for index, size in zip(place, SIZES.values()):
        at = at * size + index
    return at


def pairs(target):
    places = [()]
    for size in SIZES.values():
        places = [place + (index,) for place in places for index in range(size)]
    return [(number(place), number(target(*place))) for place in places]


def pack_kernel(at, own, out, held, came, went):
    count, rows, width = out.shape
    y, core = lax.axis_index("y"), lax.axis_index("core")
    loads, stores = [], []
    for i in range(count):
        to_x_hi, to_y = columns_of(i // 4, y, i % 4, core)
        column = pl.multiple_of((to_x_hi * 4 + to_y) * width, width)
        loads.append(pltpu.make_async_copy(own.at[pl.ds(at, rows), pl.ds(column, width)], held.at[i], came.at[i]))
        stores.append(pltpu.make_async_copy(held.at[i], out.at[i], went.at[i]))
    for load in loads[:AHEAD]:
        load.start()
    for i, (load, store) in enumerate(zip(loads, stores)):
        load.wait()
        store.start()
        if i + AHEAD < count:
            loads[i + AHEAD].start()
    for store in stores:
        store.wait()


def packed(own, at, rows):
    count = SIZES["x_lo"] * SIZES["z"]
    shape = (count, rows, own.shape[1] // count)
    return pl.pallas_call(
        functools.partial(pack_kernel, at),
        in_specs=[pl.BlockSpec(memory_space=pl.ANY)],
        out_specs=pl.BlockSpec(memory_space=pl.ANY),
        scratch_shapes=[
            pltpu.VMEM(shape, own.dtype),
            pltpu.SemaphoreType.DMA((count,)),
            pltpu.SemaphoreType.DMA((count,)),
        ],
        out_shape=jax.ShapeDtypeStruct(shape, own.dtype),
        compiler_params=pltpu.CompilerParams(vmem_limit_bytes=60 * 2**20),
        name="pack",
    )(own)


def coded(mean):
    size = jnp.exp2(jnp.abs(mean) * SCALE + SHIFT)
    return jnp.where(mean < 0, -size, size).astype(jnp.bfloat16)


def decoded(code):
    code = code.astype(jnp.float32)
    size = jnp.abs(code)
    mean = (jnp.log2(size) - SHIFT) * (1.0 / SCALE)
    mean = jnp.where(size > 2.0 ** (SHIFT + 1), mean, 0.0)
    return jnp.where(code < 0, -mean, mean)


def merged_tile(values, limits):
    high = low = None
    for value, limit in zip(values, limits):
        lifted = value + LIFT
        above = jnp.where(value > limit, lifted, 0.0)
        below = jnp.where(value < -limit, lifted, 0.0)
        high = above if high is None else high + above
        low = below if low is None else low + below
    high_count = jnp.floor(high * (1.0 / LIFT))
    low_count = jnp.ceil(low * (1.0 / LIFT))
    high_sum = high - LIFT * high_count
    low_sum = low - LIFT * low_count
    total = high_sum + low_sum
    kept = jnp.where(total > 0, high_sum, low_sum)
    count = jnp.where(total > 0, high_count, low_count)
    return jnp.where(total != 0, kept / jnp.maximum(count, 1.0), 0.0)


def mean_kernel(core, limits, tasks_same, tasks_other, same, other):
    for tasks, out in ((tasks_same, same), (tasks_other, other)):
        for row in range(0, out.shape[0], TILE_ROWS):
            for column in range(0, out.shape[1], SLICE):
                tile = pl.ds(row, TILE_ROWS), pl.ds(column, SLICE)
                values = [tasks[(t, *tile)].astype(jnp.float32) for t in range(tasks.shape[0])]
                out[tile] = coded(merged_tile(values, [limits[t] for t in range(len(values))]))


def coded_mean(tasks, limits, core):
    count, rows, width = tasks.shape
    out = jax.ShapeDtypeStruct((rows, width // 2), jnp.bfloat16)
    block = pl.BlockSpec((BLOCK_ROWS, width // 2), lambda r, *_: (r, 0))
    half = (count, BLOCK_ROWS, width // 2)
    return pl.pallas_call(
        mean_kernel,
        grid_spec=pltpu.PrefetchScalarGridSpec(
            num_scalar_prefetch=2,
            grid=(rows // BLOCK_ROWS,),
            in_specs=[
                pl.BlockSpec(half, lambda r, core, limits: (0, r, core[0])),
                pl.BlockSpec(half, lambda r, core, limits: (0, r, 1 - core[0])),
            ],
            out_specs=[block, block],
        ),
        out_shape=[out, out],
        compiler_params=pltpu.CompilerParams(vmem_limit_bytes=16 * 2**20),
        name="mean",
    )(core, limits, tasks, tasks)


def blocks_kernel(core, source, thresholds, *refs):
    blocks, outs = refs[:8], refs[8:]
    width = outs[0].shape[1]
    limits = [thresholds[source[i]] for i in range(8)]
    for half, out in enumerate(outs):
        for row in range(0, out.shape[0], TILE_ROWS):
            for first in range(0, width, SLICE):
                at = pl.multiple_of((core[0] ^ half) * width + first, SLICE)
                values = [block[pl.ds(row, TILE_ROWS), pl.ds(at, SLICE)].astype(jnp.float32) for block in blocks]
                out[pl.ds(row, TILE_ROWS), pl.ds(first, SLICE)] = coded(merged_tile(values, limits))


def coded_mean_of(blocks, source, thresholds, core):
    rows, width = blocks[0].shape
    out = jax.ShapeDtypeStruct((rows, width // 2), jnp.bfloat16)
    unit = min(rows, BLOCK_ROWS_B)
    block = pl.BlockSpec((unit, width), lambda r, *_: (r, 0))
    return pl.pallas_call(
        blocks_kernel,
        grid_spec=pltpu.PrefetchScalarGridSpec(
            num_scalar_prefetch=3,
            grid=(rows // unit,),
            in_specs=[block] * 8,
            out_specs=[pl.BlockSpec((unit, width // 2), lambda r, *_: (r, 0))] * 2,
        ),
        out_shape=[out, out],
        compiler_params=pltpu.CompilerParams(vmem_limit_bytes=16 * 2**20),
        name="mean_of_blocks",
    )(core, source, thresholds, *blocks)


def add_kernel(core, base, same, other, *rest):
    out = rest[-1]

    @pl.when(pl.program_id(0) == 0)
    def _():
        out[...] = base[...] + decoded(same[...])

    @pl.when(pl.program_id(0) == 1)
    def _():
        out[...] = base[...] + decoded(other[...])


def added(core, base, same, other, at, partial, unit):
    rows, width = same.shape
    half_rows = base.shape[0] // 2
    steps = rows // unit

    def place(h, r, core):
        return pl.multiple_of((h ^ core[0]) * half_rows + at + r * unit, 8), 0

    whole = pl.BlockSpec((pl.Element(unit), pl.Element(width)), place)
    in_specs = [
        whole,
        pl.BlockSpec((unit, width), lambda h, r, core: (r * (1 - h) + (steps - 1) * h, 0)),
        pl.BlockSpec((unit, width), lambda h, r, core: (r * h, 0)),
    ]
    args = [core, base, same, other]
    aliases = {}
    if partial is not None:
        in_specs.append(pl.BlockSpec(memory_space=pl.ANY))
        args.append(partial)
        aliases = {4: 0}
    return pl.pallas_call(
        add_kernel,
        grid_spec=pltpu.PrefetchScalarGridSpec(
            num_scalar_prefetch=1, grid=(2, steps), in_specs=in_specs, out_specs=whole
        ),
        out_shape=jax.ShapeDtypeStruct(base.shape, base.dtype),
        input_output_aliases=aliases,
        compiler_params=pltpu.CompilerParams(vmem_limit_bytes=16 * 2**20),
        name="add",
    )(*args)


def local(task_vectors, thresholds, base_weight):
    own = task_vectors[0]
    width = own.shape[1] // 8
    x_lo, z, y, core = (lax.axis_index(name) for name in ("x_lo", "z", "y", "core"))
    one = core[None].astype(jnp.int32)

    def column(hops, flip):
        to_x_lo, to_z = moved(x_lo, z, core, hops, flip)
        to_x_hi, to_y = columns_of(to_x_lo, y, to_z, core)
        return to_x_hi * 4 + to_y

    def source(hops, flip):
        from_x_lo, from_z = moved(x_lo, z, core, 4 - hops, flip)
        return from_x_lo * 4 + from_z

    sources = jnp.stack([source(*step) for step in ((0, 0), *STEPS)])

    def send(block, step):
        return lax.ppermute(block, AXES, pairs(meet(*step)))

    def send_home(codes):
        return [lax.ppermute(code, AXES, pairs(home(half))) for half, code in enumerate(codes)]

    starts = [sum(CHUNKS[:i]) for i in range(len(CHUNKS))]
    tasks = lax.all_to_all(
        packed(own, 0, CHUNKS[0]), ("x_lo", "z"), split_axis=0, concat_axis=0, tiled=True
    )
    blocks = [
        [lax.dynamic_slice(own, (at, column(*step) * width), (rows, width)) for step in ((0, 0), *STEPS)]
        for at, rows in zip(starts[1:], CHUNKS[1:])
    ]
    codes = coded_mean(tasks, thresholds, one)
    arrived, homes = None, []
    for here, early in zip(blocks, EARLY):
        if arrived is not None:
            here[1:], arrived[GATE_ON] = lax.optimization_barrier((here[1:], arrived[GATE_ON]))
            codes = coded_mean_of(arrived, sources, thresholds, one)
        sent = [send(block, step) for block, step in zip(here[1 : 1 + early], STEPS)]
        late, codes = lax.optimization_barrier((here[1 + early :], codes))
        homes.append(send_home(codes))
        arrived = here[:1] + sent + [send(block, step) for block, step in zip(late, STEPS[early:])]
    codes = coded_mean_of(arrived, sources, thresholds, one)
    homes.append(send_home(codes))
    out = None
    for (same, other), at, unit in zip(homes, starts, ADD_ROWS):
        out = added(one, base_weight, same, other, at, out, unit)
    return out


def solution(mesh):
    finer = Mesh(mesh.devices.reshape(tuple(SIZES.values())), AXES)
    ckpt, shard = ("x_lo", "z"), ("x_hi", "y", "core")
    return jax.shard_map(
        local,
        mesh=finer,
        in_specs=(P(ckpt, shard, None), P(), P(ckpt, shard)),
        out_specs=P(ckpt, shard),
        check_vma=False,
    )
```

```python
import functools

import jax
import jax.numpy as jnp
from jax import lax
from jax.experimental import pallas as pl
from jax.experimental.pallas import tpu as pltpu
from jax.sharding import Mesh, PartitionSpec as P

SIZES = dict(x_lo=2, z=4, x_hi=2, y=4, core=2)
AXES = tuple(SIZES)
CHUNKS = (160, 96)
STEPS = ((1, 0), (3, 1), (2, 0), (1, 1), (3, 0), (2, 1), (0, 1))
EARLY, GATE_ON = (4,), 4
AHEAD = 8
LIFT = 4.0
SCALE, SHIFT = 1920.0, -120.0
BLOCK_ROWS, BLOCK_ROWS_B, ADD_ROWS = 40, 48, (160, 96)
TILE_ROWS, SLICE = 8, 128


def columns_of(x_lo, y, z, core):
    return x_lo, (z - y + 2 * core + 4) % 4


def moved(x_lo, z, core, hops, flip):
    return x_lo ^ flip, (z + hops * (1 - 2 * core) + 4) % 4


def meet(hops, flip):
    def target(x_lo, z, x_hi, y, core):
        return *moved(x_lo, z, core, hops, flip), x_hi, y, core

    return target


def home(half):
    def target(x_lo, z, x_hi, y, core):
        return x_hi, y, *columns_of(x_lo, y, z, core), core ^ half

    return target


def number(place):
    at = 0
    for index, size in zip(place, SIZES.values()):
        at = at * size + index
    return at


def pairs(target):
    places = [()]
    for size in SIZES.values():
        places = [place + (index,) for place in places for index in range(size)]
    return [(number(place), number(target(*place))) for place in places]


def pack_kernel(at, own, out, held, came, went):
    count, rows, width = out.shape
    y, core = lax.axis_index("y"), lax.axis_index("core")
    loads, stores = [], []
    for i in range(count):
        to_x_hi, to_y = columns_of(i // 4, y, i % 4, core)
        column = pl.multiple_of((to_x_hi * 4 + to_y) * width, width)
        loads.append(pltpu.make_async_copy(own.at[pl.ds(at, rows), pl.ds(column, width)], held.at[i], came.at[i]))
        stores.append(pltpu.make_async_copy(held.at[i], out.at[i], went.at[i]))
    for load in loads[:AHEAD]:
        load.start()
    for i, (load, store) in enumerate(zip(loads, stores)):
        load.wait()
        store.start()
        if i + AHEAD < count:
            loads[i + AHEAD].start()
    for store in stores:
        store.wait()


def packed(own, at, rows):
    count = SIZES["x_lo"] * SIZES["z"]
    shape = (count, rows, own.shape[1] // count)
    return pl.pallas_call(
        functools.partial(pack_kernel, at),
        in_specs=[pl.BlockSpec(memory_space=pl.ANY)],
        out_specs=pl.BlockSpec(memory_space=pl.ANY),
        scratch_shapes=[
            pltpu.VMEM(shape, own.dtype),
            pltpu.SemaphoreType.DMA((count,)),
            pltpu.SemaphoreType.DMA((count,)),
        ],
        out_shape=jax.ShapeDtypeStruct(shape, own.dtype),
        compiler_params=pltpu.CompilerParams(vmem_limit_bytes=60 * 2**20),
        name="pack",
    )(own)


def coded(mean):
    size = jnp.exp2(jnp.abs(mean) * SCALE + SHIFT)
    return jnp.where(mean < 0, -size, size).astype(jnp.bfloat16)


def decoded(code):
    code = code.astype(jnp.float32)
    size = jnp.abs(code)
    mean = (jnp.log2(size) - SHIFT) * (1.0 / SCALE)
    mean = jnp.where(size > 2.0 ** (SHIFT + 1), mean, 0.0)
    return jnp.where(code < 0, -mean, mean)


def merged_tile(values, limits):
    high = low = None
    for value, limit in zip(values, limits):
        lifted = value + LIFT
        above = jnp.where(value > limit, lifted, 0.0)
        below = jnp.where(value < -limit, lifted, 0.0)
        high = above if high is None else high + above
        low = below if low is None else low + below
    high_count = jnp.floor(high * (1.0 / LIFT))
    low_count = jnp.ceil(low * (1.0 / LIFT))
    high_sum = high - LIFT * high_count
    low_sum = low - LIFT * low_count
    total = high_sum + low_sum
    kept = jnp.where(total > 0, high_sum, low_sum)
    count = jnp.where(total > 0, high_count, low_count)
    return jnp.where(total != 0, kept / jnp.maximum(count, 1.0), 0.0)


def mean_kernel(core, limits, tasks_same, tasks_other, same, other):
    for tasks, out in ((tasks_same, same), (tasks_other, other)):
        for row in range(0, out.shape[0], TILE_ROWS):
            for column in range(0, out.shape[1], SLICE):
                tile = pl.ds(row, TILE_ROWS), pl.ds(column, SLICE)
                values = [tasks[(t, *tile)].astype(jnp.float32) for t in range(tasks.shape[0])]
                out[tile] = coded(merged_tile(values, [limits[t] for t in range(len(values))]))


def coded_mean(tasks, limits, core):
    count, rows, width = tasks.shape
    out = jax.ShapeDtypeStruct((rows, width // 2), jnp.bfloat16)
    block = pl.BlockSpec((BLOCK_ROWS, width // 2), lambda r, *_: (r, 0))
    half = (count, BLOCK_ROWS, width // 2)
    return pl.pallas_call(
        mean_kernel,
        grid_spec=pltpu.PrefetchScalarGridSpec(
            num_scalar_prefetch=2,
            grid=(rows // BLOCK_ROWS,),
            in_specs=[
                pl.BlockSpec(half, lambda r, core, limits: (0, r, core[0])),
                pl.BlockSpec(half, lambda r, core, limits: (0, r, 1 - core[0])),
            ],
            out_specs=[block, block],
        ),
        out_shape=[out, out],
        compiler_params=pltpu.CompilerParams(vmem_limit_bytes=16 * 2**20),
        name="mean",
    )(core, limits, tasks, tasks)


def blocks_kernel(thresholds, *refs):
    blocks, outs = refs[:8], refs[8:]
    x_lo, z, core = (lax.axis_index(name) for name in ("x_lo", "z", "core"))
    width = outs[0].shape[1]
    limits = []
    for hops, flip in ((0, 0), *STEPS):
        from_x_lo, from_z = moved(x_lo, z, core, 4 - hops, flip)
        limits.append(thresholds[from_x_lo * 4 + from_z])
    for half, out in enumerate(outs):
        for row in range(0, out.shape[0], TILE_ROWS):
            for first in range(0, width, SLICE):
                at = pl.multiple_of((core ^ half) * width + first, SLICE)
                values = [block[pl.ds(row, TILE_ROWS), pl.ds(at, SLICE)].astype(jnp.float32) for block in blocks]
                out[pl.ds(row, TILE_ROWS), pl.ds(first, SLICE)] = coded(merged_tile(values, limits))


def coded_mean_of(blocks, thresholds):
    rows, width = blocks[0].shape
    out = jax.ShapeDtypeStruct((rows, width // 2), jnp.bfloat16)
    unit = min(rows, BLOCK_ROWS_B)
    block = pl.BlockSpec((unit, width), lambda r, *_: (r, 0))
    return pl.pallas_call(
        blocks_kernel,
        grid_spec=pltpu.PrefetchScalarGridSpec(
            num_scalar_prefetch=1,
            grid=(rows // unit,),
            in_specs=[block] * 8,
            out_specs=[pl.BlockSpec((unit, width // 2), lambda r, *_: (r, 0))] * 2,
        ),
        out_shape=[out, out],
        compiler_params=pltpu.CompilerParams(vmem_limit_bytes=16 * 2**20),
        name="mean_of_blocks",
    )(thresholds, *blocks)


def add_kernel(core, base, same, other, *rest):
    out = rest[-1]

    @pl.when(pl.program_id(0) == 0)
    def _():
        out[...] = base[...] + decoded(same[...])

    @pl.when(pl.program_id(0) == 1)
    def _():
        out[...] = base[...] + decoded(other[...])


def added(core, base, same, other, at, partial, unit):
    rows, width = same.shape
    half_rows = base.shape[0] // 2
    steps = rows // unit

    def place(h, r, core):
        return pl.multiple_of((h ^ core[0]) * half_rows + at + r * unit, 8), 0

    whole = pl.BlockSpec((pl.Element(unit), pl.Element(width)), place)
    in_specs = [
        whole,
        pl.BlockSpec((unit, width), lambda h, r, core: (r * (1 - h) + (steps - 1) * h, 0)),
        pl.BlockSpec((unit, width), lambda h, r, core: (r * h, 0)),
    ]
    args = [core, base, same, other]
    aliases = {}
    if partial is not None:
        in_specs.append(pl.BlockSpec(memory_space=pl.ANY))
        args.append(partial)
        aliases = {4: 0}
    return pl.pallas_call(
        add_kernel,
        grid_spec=pltpu.PrefetchScalarGridSpec(
            num_scalar_prefetch=1, grid=(2, steps), in_specs=in_specs, out_specs=whole
        ),
        out_shape=jax.ShapeDtypeStruct(base.shape, base.dtype),
        input_output_aliases=aliases,
        compiler_params=pltpu.CompilerParams(vmem_limit_bytes=16 * 2**20),
        name="add",
    )(*args)


def local(task_vectors, thresholds, base_weight):
    own = task_vectors[0]
    width = own.shape[1] // 8
    x_lo, z, y, core = (lax.axis_index(name) for name in ("x_lo", "z", "y", "core"))
    one = core[None].astype(jnp.int32)

    def column(hops, flip):
        to_x_lo, to_z = moved(x_lo, z, core, hops, flip)
        to_x_hi, to_y = columns_of(to_x_lo, y, to_z, core)
        return to_x_hi * 4 + to_y

    def send(block, step):
        return lax.ppermute(block, AXES, pairs(meet(*step)))

    def send_home(codes):
        return [lax.ppermute(code, AXES, pairs(home(half))) for half, code in enumerate(codes)]

    starts = [sum(CHUNKS[:i]) for i in range(len(CHUNKS))]
    tasks = lax.all_to_all(
        packed(own, 0, CHUNKS[0]), ("x_lo", "z"), split_axis=0, concat_axis=0, tiled=True
    )
    blocks = [
        [lax.dynamic_slice(own, (at, column(*step) * width), (rows, width)) for step in ((0, 0), *STEPS)]
        for at, rows in zip(starts[1:], CHUNKS[1:])
    ]
    codes = coded_mean(tasks, thresholds, one)
    arrived, homes = None, []
    for here, early in zip(blocks, EARLY):
        if arrived is not None:
            here[1:], arrived[GATE_ON] = lax.optimization_barrier((here[1:], arrived[GATE_ON]))
            codes = coded_mean_of(arrived, thresholds)
        sent = [send(block, step) for block, step in zip(here[1 : 1 + early], STEPS)]
        late, codes = lax.optimization_barrier((here[1 + early :], codes))
        homes.append(send_home(codes))
        arrived = here[:1] + sent + [send(block, step) for block, step in zip(late, STEPS[early:])]
    codes = coded_mean_of(arrived, thresholds)
    homes.append(send_home(codes))
    out = None
    for (same, other), at, unit in zip(homes, starts, ADD_ROWS):
        out = added(one, base_weight, same, other, at, out, unit)
    return out


def solution(mesh):
    finer = Mesh(mesh.devices.reshape(tuple(SIZES.values())), AXES)
    ckpt, shard = ("x_lo", "z"), ("x_hi", "y", "core")
    return jax.shard_map(
        local,
        mesh=finer,
        in_specs=(P(ckpt, shard, None), P(), P(ckpt, shard)),
        out_specs=P(ckpt, shard),
        check_vma=False,
    )
```
